32 devices in a mesh: dp: 4 (over y, x), expert: 8 (over z, core).
Axes of the slice: x: 2, y: 2, z: 4, core: 2. Of those that a mesh axis runs over, the one named last changes fastest.
Arguments:
- tokens: bfloat16 [4096, 2048], P(('dp', 'expert')), may hold values from -6 to 6
- expert_ids: int32 [4096, 4], P(('dp', 'expert')), may hold values from 0 to 7, all different within a row; in each aligned block of 128 rows (0 to 127, 128 to 255, ...) at most 80 rows name the same one
- probs: float32 [4096, 4], P(('dp', 'expert')), may hold values from 0.2 to 1
- trade: int32 [4], replicated, may hold values from 0 to 1, as said below
- gate_weight: bfloat16 [8, 2048, 768], P('expert'), may hold values from -0.125 to 0.125
- up_weight: bfloat16 [8, 2048, 768], P('expert'), may hold values from -0.125 to 0.125
- down_weight: bfloat16 [8, 768, 2048], P('expert'), may hold values from -0.21875 to 0.21875
- out_grad: bfloat16 [4096, 2048], P(('dp', 'expert')), may hold values from -0.29882812 to 0.29882812
Outputs:
- combined: bfloat16 [4096, 2048], P(('dp', 'expert'))
- gate_grad: bfloat16 [8, 2048, 768], P('expert', 'dp')
- up_grad: bfloat16 [8, 2048, 768], P('expert', 'dp')
- down_grad: bfloat16 [8, 768, 2048], P('expert', None, 'dp')
The draws below stay inside these ranges and needn't reach their ends.
Inputs may be any that keep to these rules, and one draw needn't show every extreme that they name: `trade`: index k below 4 pairs expert index k with k + 4; at least one pair trades and at least one does not. `expert_ids`: each row names 4 different experts. Within the 128 rows of one device no expert is named by more than 80 rows, a bound that some block reaches.
All inputs are finite; a program needn't handle non-finite values.
Results may differ from the reference program's by a relative error of at most 0.0095.
Values may be sent and summed in bfloat16 or wider, within the bound.
A program may use at most 128 MiB of HBM per device.

```python
import math
import jax
import jax.numpy as jnp
import numpy as np
from jax import lax

D = 2048
FF = 768
TOPK = 4
TOK_DEV = 128
EXPERTS = 8
CAP = 80
HALF = 4
ROWS = 640
TOKENS = 4096
N_DP = 4
N_EXPERT = 8


def draw_trade(key, part):
    coins = jax.random.randint(jax.random.fold_in(key, 4391), (HALF,), 0, 2, dtype=jnp.int32)
    order = jax.random.permutation(jax.random.fold_in(key, 5821), HALF)
    coins = coins.at[order[0]].set(1)
    coins = coins.at[order[1]].set(0)
    return coins.astype(jnp.int32)


def steps_of(rng, shape, split, low, top_value):
    level, own = 1.0, jax.random.fold_in(rng, 6)
    for position, blocks in split:
        steps = jnp.exp(jax.random.uniform(jax.random.fold_in(own, position), (blocks,), jnp.float32, low / len(split), top_value / len(split)))
        level = level * jnp.repeat(steps, shape[position] // blocks).reshape([-1 if axis == position else 1 for axis in range(len(shape))])
    return level


def assign_block(key, own, number, rows, amount, top, bound, skew):
    order = jax.random.permutation(key, amount)
    crowded, usual = shares(amount, rows * top, bound, skew, True), shares(amount, rows * top, bound, skew, False)
    places = jnp.arange(amount)

    def named(lengths, offset_by):
        used = int((lengths > 0).sum())
        fixed = max(1, used // 4)
        passed = fixed + (places - fixed + offset_by * (used - fixed)) % max(1, amount - fixed)
        return jnp.zeros((amount,), jnp.int32).at[order[jnp.where(places < fixed, places, passed)]].set(jnp.asarray(lengths, jnp.int32))

    lengths = jnp.where(number % 4 == 0, named(crowded, number // 4), named(usual, number - number // 4 - 1))
    mixed = jax.random.permutation(jax.random.fold_in(own, 3), amount)
    source_of, sink = mixed[0:amount // 2 * 2:2], mixed[1:amount // 2 * 2:2]
    slack = jnp.minimum(lengths[source_of] - 1, bound - lengths[sink]) // 2
    slack = jnp.where((source_of == order[0]) | (sink == order[0]) | (lengths[sink] == 0), 0, jnp.maximum(slack, 0))
    passed = jax.random.randint(jax.random.fold_in(own, 4), (amount // 2,), 0, 1 << 20) % (slack + 1)
    lengths = lengths.at[source_of].add(-passed).at[sink].add(passed)
    members = jnp.searchsorted(jnp.cumsum(lengths), jnp.arange(rows * top), side="right").astype(jnp.int32)
    listing = members.reshape(top, rows).T
    listing = listing[jax.random.permutation(jax.random.fold_in(own, 1), rows)]
    offset_by = jax.random.randint(jax.random.fold_in(own, 2), (rows, 1), 0, top)
    return jnp.take_along_axis(listing, (jnp.arange(top)[None, :] + offset_by) % top, axis=1)


def shares(number_of, total, limit, slope, full):
    portions = [(1 << 20) // math.isqrt(standing ** slope) + 1 for standing in range(1, number_of + 1)]
    largest = limit if full else min(limit, max(-(-total // number_of), total * portions[0] // sum(portions)))
    least = 1 if total - largest >= number_of - 1 else 0
    counts, rest = [largest] + [least] * (number_of - 1), total - largest - least * (number_of - 1)
    while rest > 0:
        movable = [i for i in range(1, number_of) if counts[i] < largest] or [i for i in range(1, number_of) if counts[i] < limit]
        pool, budget = sum([portions[i] for i in movable]), rest
        for i in movable:
            more = min(limit - counts[i], max(1, budget * portions[i] // pool), rest)
            counts[i] = counts[i] + more
            rest = rest - more
    return np.array(counts)


def normal_values(rng, dims, deviation, limit, cuts=(), kind=jnp.bfloat16):
    values = jax.random.normal(rng, dims, jnp.float32) * deviation
    if len(cuts) > 0:
        values = steps_of(rng, dims, cuts, -0.22, 0.18) * values
    return jnp.clip(values, min=-limit, max=limit).astype(kind)


def setup_inputs(seed: int = 0) -> dict:
    key_list = jax.random.split(jax.random.key(seed), 9)
    tokens = normal_values(key_list[0], (TOKENS, D), 1.0, 6.0, ((0, 32),))
    expert_ids_keys = jax.random.split(jax.random.fold_in(key_list[1], 1), TOKENS // TOK_DEV)
    expert_ids_turns = jax.random.permutation(jax.random.fold_in(key_list[1], 3), TOKENS // TOK_DEV)
    expert_ids = jax.vmap(lambda own, number: assign_block(jax.random.fold_in(key_list[1], 2), own, number, TOK_DEV, EXPERTS, TOPK, CAP, 2))(expert_ids_keys, expert_ids_turns).reshape((TOKENS, TOPK))
    probs = jnp.clip(0.2 + 0.8 * jax.random.uniform(key_list[2], (TOKENS, TOPK), jnp.float32) ** steps_of(key_list[2], (TOKENS, TOPK), ((0, 32),), -0.2, 0.2), 0.2, 1.0)
    trade = draw_trade(jax.random.fold_in(key_list[8], 71), 0)
    gate_weight = normal_values(key_list[4], (EXPERTS, D, FF), D ** -0.5, 0.125, ((0, 8),))
    up_weight = normal_values(key_list[5], (EXPERTS, D, FF), D ** -0.5, 0.125, ((0, 8),))
    down_weight = normal_values(key_list[6], (EXPERTS, FF, D), FF ** -0.5, 0.21875, ((0, 8),))
    out_grad = normal_values(key_list[7], (TOKENS, D), 0.05, 0.29882812, ((0, 32),))
    return {"tokens": tokens, "expert_ids": expert_ids, "probs": probs, "trade": trade, "gate_weight": gate_weight, "up_weight": up_weight, "down_weight": down_weight, "out_grad": out_grad}


def rounded(value):
    return lax.optimization_barrier(value.astype(jnp.bfloat16)).astype(jnp.float32)


def slot_numbers(expert_ids):
    sources = N_DP * N_EXPERT
    pair_count = TOK_DEV * TOPK
    chosen = expert_ids.reshape(sources, pair_count).astype(jnp.int32)
    numbers = jnp.arange(EXPERTS, dtype=jnp.int32)
    onehot = (chosen[:, :, None] == numbers[None, None, :]).astype(jnp.int32)
    earlier = jnp.cumsum(onehot, axis=1) - onehot
    placed = jnp.sum(earlier * onehot, axis=2).astype(jnp.int32)
    return (chosen * CAP + placed).astype(jnp.int32)


def reference(tokens, expert_ids, probs, trade, gate_weight, up_weight, down_weight, out_grad):
    sources = N_DP * N_EXPERT
    pair_count = TOK_DEV * TOPK
    slots = slot_numbers(expert_ids)
    pair_ids = jnp.arange(sources * pair_count, dtype=jnp.int32).reshape(sources, pair_count)
    source_ids = jnp.arange(sources, dtype=jnp.int32)[:, None]
    table = jnp.full((sources, EXPERTS * CAP), -1, jnp.int32).at[source_ids, slots].set(pair_ids)
    table = table.reshape(sources, EXPERTS, CAP).transpose(1, 0, 2).reshape(EXPERTS, sources * CAP)
    numbers = jnp.arange(EXPERTS, dtype=jnp.int32)
    halfway = EXPERTS // 2
    owners = jnp.where(trade[numbers % halfway] == 1, jnp.bitwise_xor(numbers, halfway), numbers).astype(jnp.int32)
    prob_flat = probs.reshape(-1)

    def expert_step(combined_sum, inputs):
        pairs, owner = inputs
        live = pairs >= 0
        safe_pairs = jnp.where(live, pairs, 0).astype(jnp.int32)
        token_rows = (safe_pairs // TOPK).astype(jnp.int32)
        weight_col = jnp.where(live, prob_flat[safe_pairs], jnp.zeros((), jnp.float32))
        expert_rows = jnp.where(live[:, None], tokens[token_rows], jnp.zeros((), jnp.bfloat16))
        w_gate = gate_weight[owner]
        w_up = up_weight[owner]
        w_down = down_weight[owner]
        gate_act = jnp.dot(expert_rows, w_gate, preferred_element_type=jnp.float32)
        up_act = jnp.dot(expert_rows, w_up, preferred_element_type=jnp.float32)
        sigma = jax.nn.sigmoid(gate_act)
        silu_gate = gate_act * sigma
        hidden = (silu_gate * up_act).astype(jnp.bfloat16)
        expert_out = jnp.dot(hidden, w_down, preferred_element_type=jnp.float32).astype(jnp.bfloat16)
        combined_sum = combined_sum.at[token_rows].add(weight_col[:, None] * expert_out.astype(jnp.float32))
        out_rows = (weight_col[:, None] * out_grad[token_rows].astype(jnp.float32)).astype(jnp.bfloat16)
        hidden_grad = jnp.dot(out_rows, w_down.T, preferred_element_type=jnp.float32)
        gate_back = (hidden_grad * up_act * (sigma * (1.0 + gate_act * (1.0 - sigma)))).astype(jnp.bfloat16)
        up_back = (hidden_grad * silu_gate).astype(jnp.bfloat16)
        gate_total = jnp.zeros((D, FF), jnp.float32)
        up_total = jnp.zeros((D, FF), jnp.float32)
        down_total = jnp.zeros((FF, D), jnp.float32)
        for replica in range(N_DP):
            lower = replica * ROWS
            part_rows = expert_rows[lower:lower + ROWS]
            gate_total = gate_total + rounded(jnp.dot(part_rows.T, gate_back[lower:lower + ROWS], preferred_element_type=jnp.float32))
            up_total = up_total + rounded(jnp.dot(part_rows.T, up_back[lower:lower + ROWS], preferred_element_type=jnp.float32))
            down_total = down_total + rounded(jnp.dot(hidden[lower:lower + ROWS].T, out_rows[lower:lower + ROWS], preferred_element_type=jnp.float32))
        return combined_sum, (gate_total.astype(jnp.bfloat16), up_total.astype(jnp.bfloat16), down_total.astype(jnp.bfloat16))

    combined_sum, grads = lax.scan(expert_step, jnp.zeros((TOKENS, D), jnp.float32), (table, owners))
    return (combined_sum.astype(jnp.bfloat16), grads[0][owners], grads[1][owners], grads[2][owners])
```

```python
import jax
import jax.numpy as jnp
from jax import lax
from jax.sharding import PartitionSpec as P


def sparse_local(tokens, expert_ids, probs, trade, gate_weight, up_weight, down_weight, out_grad):
    tok_count, model_width = tokens.shape
    top_count = expert_ids.shape[1]
    hidden_width = gate_weight.shape[2]
    experts = lax.axis_size("expert")
    capacity = 5 * tok_count * top_count // (4 * experts)
    halfway = experts // 2
    chosen = expert_ids.reshape(-1)
    numbers = jnp.arange(experts, dtype=jnp.int32)
    onehot = (chosen[:, None] == numbers[None, :]).astype(jnp.int32)
    earlier = jnp.cumsum(onehot, axis=0) - onehot
    slots = chosen * capacity + jnp.sum(earlier * onehot, axis=1)
    owners = jnp.where(trade[numbers % halfway] == 1, jnp.bitwise_xor(numbers, halfway), numbers)
    pair_tokens = jnp.arange(chosen.shape[0], dtype=jnp.int32) // top_count
    send_rows = (
        jnp.zeros((experts * capacity, model_width), jnp.bfloat16)
        .at[slots]
        .set(tokens[pair_tokens])
    )
    send_rows = send_rows.reshape(experts, capacity, model_width)
    out_pairs = (probs[:, :, None] * out_grad[:, None, :].astype(jnp.float32)).astype(jnp.bfloat16)
    send_grads = (
        jnp.zeros((experts * capacity, model_width), jnp.bfloat16)
        .at[slots]
        .set(out_pairs.reshape(-1, model_width))
    )
    send_grads = send_grads.reshape(experts, capacity, model_width)
    send_rows = send_rows[owners]
    send_grads = send_grads[owners]
    w_gate = gate_weight[0]
    w_up = up_weight[0]
    w_down = down_weight[0]
    arrived = lax.all_to_all(send_rows, "expert", split_axis=0, concat_axis=0, tiled=True)
    lead = arrived.shape[:2]
    flat_rows = arrived.reshape(-1, model_width)
    gate_act = jnp.dot(flat_rows, w_gate, preferred_element_type=jnp.float32)
    up_act = jnp.dot(flat_rows, w_up, preferred_element_type=jnp.float32)
    forward_hidden = (gate_act * jax.nn.sigmoid(gate_act) * up_act).astype(jnp.bfloat16)
    expert_out = jnp.dot(forward_hidden, w_down, preferred_element_type=jnp.float32).astype(
        jnp.bfloat16
    )
    arrived, expert_out, hidden, gate_act, up_act = (
        arrived,
        expert_out.reshape(lead + (model_width,)),
        forward_hidden.reshape(lead + (hidden_width,)),
        gate_act.reshape(lead + (hidden_width,)),
        up_act.reshape(lead + (hidden_width,)),
    )
    returned = lax.all_to_all(expert_out, "expert", split_axis=0, concat_axis=0, tiled=True)
    out_rows = lax.all_to_all(send_grads, "expert", split_axis=0, concat_axis=0, tiled=True)
    returned = returned[owners]
    picked = returned.reshape(-1, model_width)[slots].reshape(tok_count, top_count, model_width)
    combined = jnp.sum(probs[:, :, None] * picked.astype(jnp.float32), axis=1).astype(jnp.bfloat16)
    expert_rows = arrived.reshape(-1, model_width)
    out_rows = out_rows.reshape(-1, model_width)
    hidden = hidden.reshape(-1, hidden_width)
    gate_act = gate_act.reshape(-1, hidden_width)
    up_act = up_act.reshape(-1, hidden_width)
    hidden_grad = lax.dot_general(
        out_rows, w_down, (((1,), (1,)), ((), ())), preferred_element_type=jnp.float32
    )
    sigma = jax.nn.sigmoid(gate_act)
    gate_back = (hidden_grad * up_act * (sigma * (1.0 + gate_act * (1.0 - sigma)))).astype(
        jnp.bfloat16
    )
    up_back = (hidden_grad * (gate_act * sigma)).astype(jnp.bfloat16)
    both_back = jnp.concatenate([gate_back, up_back], axis=1)
    first = lax.dot_general(
        expert_rows, both_back, (((0,), (0,)), ((), ())), preferred_element_type=jnp.float32
    )
    second = lax.dot_general(
        out_rows, hidden, (((0,), (0,)), ((), ())), preferred_element_type=jnp.float32
    )
    summed = lax.psum_scatter(
        jnp.concatenate([first, second], axis=1).astype(jnp.bfloat16),
        "dp",
        scatter_dimension=0,
        tiled=True,
    )
    gate_part = summed[:, :hidden_width]
    up_part = summed[:, hidden_width : 2 * hidden_width]
    down_part = summed[:, 2 * hidden_width :].T
    return (combined, gate_part[None], up_part[None], down_part[None])


def dense_local(tokens, expert_ids, probs, trade, gate_weight, up_weight, down_weight, out_grad):
    hidden_width = gate_weight.shape[2]
    experts = lax.axis_size("expert")
    halfway = experts // 2
    me = lax.axis_index("expert")
    mine = jnp.where(trade[me % halfway] == 1, jnp.bitwise_xor(me, halfway), me)
    rows = lax.all_gather(tokens, "expert", axis=0, tiled=True)
    ids = lax.all_gather(expert_ids, "expert", axis=0, tiled=True)
    weights = lax.all_gather(probs, "expert", axis=0, tiled=True)
    grads = lax.all_gather(out_grad, "expert", axis=0, tiled=True)
    weight = jnp.sum(jnp.where(ids == mine, weights, 0.0), axis=1, keepdims=True)
    w_gate = gate_weight[0]
    w_up = up_weight[0]
    w_down = down_weight[0]
    gate_act = jnp.dot(rows, w_gate, preferred_element_type=jnp.float32)
    up_act = jnp.dot(rows, w_up, preferred_element_type=jnp.float32)
    sigma = jax.nn.sigmoid(gate_act)
    hidden = (gate_act * sigma * up_act).astype(jnp.bfloat16)
    expert_out = jnp.dot(hidden, w_down, preferred_element_type=jnp.float32)
    part = (weight * expert_out).astype(jnp.bfloat16)
    out_rows = (weight * grads.astype(jnp.float32)).astype(jnp.bfloat16)
    hidden_grad = lax.dot_general(
        out_rows, w_down, (((1,), (1,)), ((), ())), preferred_element_type=jnp.float32
    )
    gate_back = (hidden_grad * up_act * (sigma * (1.0 + gate_act * (1.0 - sigma)))).astype(
        jnp.bfloat16
    )
    up_back = (hidden_grad * (gate_act * sigma)).astype(jnp.bfloat16)
    both_back = jnp.concatenate([gate_back, up_back], axis=1)
    first = lax.dot_general(
        rows, both_back, (((0,), (0,)), ((), ())), preferred_element_type=jnp.float32
    )
    second = lax.dot_general(
        out_rows, hidden, (((0,), (0,)), ((), ())), preferred_element_type=jnp.float32
    )
    summed = lax.psum_scatter(
        jnp.concatenate([first, second], axis=1).astype(jnp.bfloat16),
        "dp",
        scatter_dimension=0,
        tiled=True,
    )
    combined = lax.psum_scatter(part, "expert", scatter_dimension=0, tiled=True)
    gate_part = summed[:, :hidden_width]
    up_part = summed[:, hidden_width : 2 * hidden_width]
    down_part = summed[:, 2 * hidden_width :].T
    return (combined, gate_part[None], up_part[None], down_part[None])


def local(tokens, expert_ids, *rest):
    capacity = 5 * tokens.shape[0] * expert_ids.shape[1] // (4 * lax.axis_size("expert"))
    if tokens.shape[0] <= 2 * capacity:
        return dense_local(tokens, expert_ids, *rest)
    return sparse_local(tokens, expert_ids, *rest)


def solution(mesh):
    return jax.shard_map(
        local,
        mesh=mesh,
        in_specs=(
            P(("dp", "expert"), None),
            P(("dp", "expert"), None),
            P(("dp", "expert"), None),
            P(),
            P("expert", None, None),
            P("expert", None, None),
            P("expert", None, None),
            P(("dp", "expert"), None),
        ),
        out_specs=(
            P(("dp", "expert"), None),
            P("expert", "dp", None),
            P("expert", "dp", None),
            P("expert", None, "dp"),
        ),
        check_vma=False,
    )
```

```python
import functools
import jax
import jax.numpy as jnp
from jax import lax
from jax.experimental import pallas as pl
from jax.experimental.pallas import tpu as pltpu
from jax.sharding import PartitionSpec as P


def sparse_local(tokens, expert_ids, probs, trade, gate_weight, up_weight, down_weight, out_grad):
    tok_count, model_width = tokens.shape
    top_count = expert_ids.shape[1]
    hidden_width = gate_weight.shape[2]
    experts = lax.axis_size("expert")
    capacity = 5 * tok_count * top_count // (4 * experts)
    halfway = experts // 2
    chosen = expert_ids.reshape(-1)
    numbers = jnp.arange(experts, dtype=jnp.int32)
    onehot = (chosen[:, None] == numbers[None, :]).astype(jnp.int32)
    earlier = jnp.cumsum(onehot, axis=0) - onehot
    slots = chosen * capacity + jnp.sum(earlier * onehot, axis=1)
    owners = jnp.where(trade[numbers % halfway] == 1, jnp.bitwise_xor(numbers, halfway), numbers)
    pair_tokens = jnp.arange(chosen.shape[0], dtype=jnp.int32) // top_count
    send_rows = (
        jnp.zeros((experts * capacity, model_width), jnp.bfloat16)
        .at[slots]
        .set(tokens[pair_tokens])
    )
    send_rows = send_rows.reshape(experts, capacity, model_width)
    out_pairs = (probs[:, :, None] * out_grad[:, None, :].astype(jnp.float32)).astype(jnp.bfloat16)
    send_grads = (
        jnp.zeros((experts * capacity, model_width), jnp.bfloat16)
        .at[slots]
        .set(out_pairs.reshape(-1, model_width))
    )
    send_grads = send_grads.reshape(experts, capacity, model_width)
    send_rows = send_rows[owners]
    send_grads = send_grads[owners]
    w_gate = gate_weight[0]
    w_up = up_weight[0]
    w_down = down_weight[0]
    arrived = lax.all_to_all(send_rows, "expert", split_axis=0, concat_axis=0, tiled=True)
    lead = arrived.shape[:2]
    flat_rows = arrived.reshape(-1, model_width)
    gate_act = jnp.dot(flat_rows, w_gate, preferred_element_type=jnp.float32)
    up_act = jnp.dot(flat_rows, w_up, preferred_element_type=jnp.float32)
    forward_hidden = (gate_act * jax.nn.sigmoid(gate_act) * up_act).astype(jnp.bfloat16)
    expert_out = jnp.dot(forward_hidden, w_down, preferred_element_type=jnp.float32).astype(
        jnp.bfloat16
    )
    arrived, expert_out, hidden, gate_act, up_act = (
        arrived,
        expert_out.reshape(lead + (model_width,)),
        forward_hidden.reshape(lead + (hidden_width,)),
        gate_act.reshape(lead + (hidden_width,)),
        up_act.reshape(lead + (hidden_width,)),
    )
    returned = lax.all_to_all(expert_out, "expert", split_axis=0, concat_axis=0, tiled=True)
    out_rows = lax.all_to_all(send_grads, "expert", split_axis=0, concat_axis=0, tiled=True)
    returned = returned[owners]
    picked = returned.reshape(-1, model_width)[slots].reshape(tok_count, top_count, model_width)
    combined = jnp.sum(probs[:, :, None] * picked.astype(jnp.float32), axis=1).astype(jnp.bfloat16)
    expert_rows = arrived.reshape(-1, model_width)
    out_rows = out_rows.reshape(-1, model_width)
    hidden = hidden.reshape(-1, hidden_width)
    gate_act = gate_act.reshape(-1, hidden_width)
    up_act = up_act.reshape(-1, hidden_width)
    hidden_grad = lax.dot_general(
        out_rows, w_down, (((1,), (1,)), ((), ())), preferred_element_type=jnp.float32
    )
    sigma = jax.nn.sigmoid(gate_act)
    gate_back = (hidden_grad * up_act * (sigma * (1.0 + gate_act * (1.0 - sigma)))).astype(
        jnp.bfloat16
    )
    up_back = (hidden_grad * (gate_act * sigma)).astype(jnp.bfloat16)
    both_back = jnp.concatenate([gate_back, up_back], axis=1)
    first = lax.dot_general(
        expert_rows, both_back, (((0,), (0,)), ((), ())), preferred_element_type=jnp.float32
    )
    second = lax.dot_general(
        out_rows, hidden, (((0,), (0,)), ((), ())), preferred_element_type=jnp.float32
    )
    summed = lax.psum_scatter(
        jnp.concatenate([first, second], axis=1).astype(jnp.bfloat16),
        "dp",
        scatter_dimension=0,
        tiled=True,
    )
    gate_part = summed[:, :hidden_width]
    up_part = summed[:, hidden_width : 2 * hidden_width]
    down_part = summed[:, 2 * hidden_width :].T
    return (combined, gate_part[None], up_part[None], down_part[None])


def layer_kernel(
    tokens, grads, weights, wg_hbm, wu_hbm, wd_hbm, combined, gate_out, up_out, down_out,
    rows, cots, wts, wg, wu, wd, wcol, hidden, back, acc, pairs, part, sib_part, far_part,
    gu, dn, gu_x, gu_y, dn_x, dn_y, gu_two, dn_two,
    load_sem, tok_send, tok_sib, tok_recv, cot_send, cot_sib, cot_recv, wt_send, wt_recv,
    part_sib, part_sib_recv, part_send, part_recv, red_send, red_recv,
):
    f32 = jnp.float32
    bf16 = jnp.bfloat16
    experts = lax.axis_size("expert")
    chips = experts // 2
    last = chips - 1
    replicas = lax.axis_size("dp")
    count, width = tokens.shape
    share = width // replicas
    ff = wg.shape[1]
    me = lax.axis_index("expert")
    z = me // 2
    c = me % 2
    d = lax.axis_index("dp")
    dx = (d // 2) * 2 + (1 - d % 2)
    dy = (1 - d // 2) * 2 + d % 2
    dd = 3 - d
    upper = z // (chips // 2)
    zm = z * (1 - upper) + (last - z) * upper
    sibling = z * 2 + (1 - c)
    inner = zm == 1

    def at_chip(m):
        return m * (1 - upper) + (last - m) * upper

    def other(q):
        return at_chip(jnp.where(q == 0, zm, jnp.where(q == 1, 1 - zm, q)))

    def owner_of(p):
        return jnp.where(p == 0, dd, jnp.where(p == 1, dx, jnp.where(p == 2, dy, d)))

    def lanes(p):
        return pl.ds(pl.multiple_of(owner_of(p) * share, share), share)

    def remote(src, dst, ssem, rsem, axis, to):
        return pltpu.make_async_remote_copy(
            src_ref=src, dst_ref=dst, send_sem=ssem, recv_sem=rsem,
            device_id={axis: to}, device_id_type=pl.DeviceIdType.MESH,
        )

    loads = [
        pltpu.make_async_copy(wg_hbm, wg, load_sem.at[0]),
        pltpu.make_async_copy(wu_hbm, wu, load_sem.at[1]),
        pltpu.make_async_copy(wd_hbm, wd, load_sem.at[2]),
        pltpu.make_async_copy(tokens, rows.at[me], load_sem.at[3]),
        pltpu.make_async_copy(weights, wts.at[me], load_sem.at[4]),
    ]
    loads[3].start()
    loads[4].start()

    def cot_load(p):
        return pltpu.make_async_copy(grads.at[:, lanes(p)], cots.at[p, me], load_sem.at[5 + p])

    for load in loads[:3]:
        load.start()
    for p in range(replicas):
        cot_load(p).start()

    barrier = pltpu.get_barrier_semaphore()
    for r in range(1, experts):
        pl.semaphore_signal(
            barrier, inc=1, device_id={"expert": (me + r) % experts},
            device_id_type=pl.DeviceIdType.MESH,
        )
    for to in (dx, dy):
        pl.semaphore_signal(
            barrier, inc=1, device_id={"dp": to}, device_id_type=pl.DeviceIdType.MESH
        )
    pl.semaphore_wait(barrier, experts + 1)

    def tok_copy(q):
        to = other(q) * 2 + c
        return remote(tokens, rows.at[me], tok_send.at[q], tok_recv.at[me], "expert", to)

    def cot_copy(p, q):
        to = other(q) * 2 + c
        return remote(
            grads.at[:, lanes(p)], cots.at[p, me], cot_send.at[p, q], cot_recv.at[p, me],
            "expert", to,
        )

    def each_target(fn):
        for q in range(1, chips):
            if q < last:
                fn(q)
            else:
                pl.when(inner)(functools.partial(fn, q))

    each_target(lambda q: tok_copy(q).start())

    def wt_copy(r):
        return remote(
            weights, wts.at[me], wt_send.at[r], wt_recv.at[me], "expert", (me + r) % experts
        )

    for r in range(1, experts):
        wt_copy(r).start()

    end = at_chip(0) * 2 + c

    def tok_from(slot):
        return remote(rows.at[slot], rows.at[slot], tok_send.at[0], tok_recv.at[slot], "expert", end)

    def tok_to_sib(zp):
        slot = zp * 2 + c
        return remote(
            rows.at[slot], rows.at[slot], tok_sib.at[zp], tok_recv.at[slot], "expert", sibling
        )

    def cot_from(p, slot):
        ref = cots.at[p, slot]
        return remote(ref, ref, cot_send.at[p, 0], cot_recv.at[p, slot], "expert", end)

    def cot_to_sib(p, zp):
        slot = zp * 2 + c
        ref = cots.at[p, slot]
        return remote(ref, ref, cot_sib.at[p, zp], cot_recv.at[p, slot], "expert", sibling)

    def part_to_sib(zp):
        return remote(
            part.at[zp * 2 + (1 - c)], sib_part.at[zp], part_sib.at[zp], part_sib_recv.at[zp],
            "expert", sibling,
        )

    loads[4].wait()
    for r in range(1, experts):
        slot = (me + r) % experts
        remote(weights, wts.at[slot], wt_send.at[r], wt_recv.at[slot], "expert", slot).wait_recv()
    eye = lax.broadcasted_iota(jnp.int32, (count, count), 0) == lax.broadcasted_iota(
        jnp.int32, (count, count), 1
    )
    for slot in range(experts):
        row = jnp.broadcast_to(wts[slot, pl.ds(me, 1), :], (count, count))
        column = jnp.sum(jnp.where(eye, row, 0.0), axis=1, keepdims=True)
        wcol[pl.ds(slot * count, count), :] = jnp.broadcast_to(column, (count, wcol.shape[1]))

    pair = 2 * count

    @pl.loop(0, chips)
    def _(q):
        zp = other(q)

        @pl.when(q == 0)
        def _():
            loads[3].wait()

        @pl.when(q > 0)
        def _():
            tok_from(zp * 2 + c).wait_recv()

        tok_to_sib(zp).start()

        @pl.when(jnp.logical_and(inner, q == last))
        def _():
            tok_from(zp * 2 + c).start()

        @pl.when(q == 0)
        def _():
            for load in loads[:3]:
                load.wait()

        @pl.when(q == last)
        def _():
            for p in range(2):
                each_target(lambda q: cot_copy(p, q).start())

        tok_from(zp * 2 + (1 - c)).wait_recv()
        where = pl.ds(pl.multiple_of(zp * pair, pair), pair)
        x = rows[pl.ds(zp * 2, 2)].reshape(pair, width)
        tile = ff // 3

        @pl.loop(0, 3)
        def _(n):
            cols = pl.ds(pl.multiple_of(n * tile, tile), tile)
            g = jnp.dot(x, wg[:, cols], preferred_element_type=f32)
            u = jnp.dot(x, wu[:, cols], preferred_element_type=f32)
            sigma = jax.nn.sigmoid(g)
            silu = g * sigma
            hidden[where, cols] = (silu * u).astype(bf16)
            back[where, cols] = (u * (sigma * (1.0 + g * (1.0 - sigma)))).astype(bf16)
            back[where, pl.ds(pl.multiple_of(ff + n * tile, tile), tile)] = silu.astype(bf16)

        @pl.loop(0, replicas)
        def _(n):
            cols = pl.ds(pl.multiple_of(n * share, share), share)
            o = jnp.dot(hidden[where, :], wd[:, cols], preferred_element_type=f32)
            o = (o * wcol[where, 0:1]).astype(bf16)
            part[zp * 2, :, cols] = o[:count]
            part[zp * 2 + 1, :, cols] = o[count:]

        part_to_sib(zp).start()

    half = share // 2
    fhalf = ff // 2

    def reduce_copy(step, wide):
        send, far = (gu, (gu_x, gu_y, gu_two)) if wide else (dn, (dn_x, dn_y, dn_two))
        h = half if wide else fhalf
        lo, hi = pl.ds(0, h), pl.ds(h, h)
        src, dst, axis_to = {
            0: (send.at[0, lo], far[0].at[0], dx),
            1: (send.at[0, hi], far[1].at[0], dy),
            2: (send.at[1, lo], far[0].at[1], dx),
            3: (send.at[2, hi], far[1].at[1], dy),
            4: (send.at[2, lo], far[2].at[0], dy),
            5: (send.at[1, hi], far[2].at[1], dx),
        }[step]
        k = step + 6 * int(wide)
        return remote(src, dst, red_send.at[k], red_recv.at[k], "dp", axis_to)

    def reduce_step(p, wide):
        send, far = (gu, (gu_x, gu_y)) if wide else (dn, (dn_x, dn_y))
        h = half if wide else fhalf
        lo, hi = pl.ds(0, h), pl.ds(h, h)

        @pl.when(p == 0)
        def _():
            reduce_copy(0, wide).start()
            reduce_copy(1, wide).start()

        @pl.when(p == 1)
        def _():
            reduce_copy(2, wide).start()

        @pl.when(p == 2)
        def _():
            reduce_copy(3, wide).start()

        @pl.when(p == 3)
        def _():
            reduce_copy(0, wide).wait_recv()
            send[2, lo] = (send[2, lo].astype(f32) + far[0][0].astype(f32)).astype(bf16)
            reduce_copy(4, wide).start()
            reduce_copy(1, wide).wait_recv()
            send[1, hi] = (send[1, hi].astype(f32) + far[1][0].astype(f32)).astype(bf16)
            reduce_copy(5, wide).start()

    @pl.loop(0, replicas)
    def _(p):
        for q in range(chips):
            zp = other(q)
            if q == 0:
                cot_load(p).wait()
            else:
                cot_from(p, zp * 2 + c).wait_recv()
            cot_to_sib(p, zp).start()
            if q == last:

                @pl.when(inner)
                def _():
                    cot_from(p, zp * 2 + c).start()

        @pl.when(p < replicas - 2)
        def _():
            each_target(lambda q: cot_copy(p + 2, q).start())

        for zp in range(chips):
            cot_from(p, zp * 2 + (1 - c)).wait_recv()
        for slot in range(experts):
            where = pl.ds(slot * count, count)
            pairs[where, :] = (wcol[where, 0:1] * cots[p, slot].astype(f32)).astype(bf16)
        tile = ff // 3

        @pl.loop(0, 3)
        def _(n):
            cols = pl.ds(pl.multiple_of(n * tile, tile), tile)
            dn[p, cols, :] = lax.dot_general(
                hidden[:, cols], pairs[...], (((0,), (0,)), ((), ())), preferred_element_type=f32
            ).astype(bf16)

        reduce_step(p, False)

        @pl.loop(0, 3)
        def _(n):
            cols = pl.ds(pl.multiple_of(n * tile, tile), tile)
            more = lax.dot_general(
                pairs[...], wd[cols, lanes(p)], (((1,), (1,)), ((), ())),
                preferred_element_type=f32,
            )
            acc[:, cols] = jnp.where(p == 0, more, acc[:, cols] + more)

    @pl.loop(0, experts)
    def _(n):
        where = pl.ds(pl.multiple_of(n * count, count), count)
        back[where, :ff] = (acc[where, :] * back[where, :ff].astype(f32)).astype(bf16)
        back[where, ff:] = (acc[where, :] * back[where, ff:].astype(f32)).astype(bf16)

    def part_copy(q):
        zp = other(q)
        return remote(
            part.at[zp * 2 + c], far_part.at[z], part_send.at[q], part_recv.at[z], "expert",
            zp * 2 + c,
        )

    for q in (0,) + tuple(range(last, 0, -1)):
        zp = other(q)
        remote(
            part.at[zp * 2 + (1 - c)], sib_part.at[zp], part_sib.at[zp], part_sib_recv.at[zp],
            "expert", sibling,
        ).wait_recv()
        part[zp * 2 + c] = (
            part[zp * 2 + c].astype(f32) + sib_part[zp].astype(f32)
        ).astype(bf16)
        if q > 0:
            part_copy(q).start()

    @pl.loop(0, replicas)
    def _(p):
        for h in range(2):
            cols = pl.ds(pl.multiple_of(owner_of(p) * share + h * half, half), half)
            lhs = rows[:, :, cols].reshape(experts * count, half)
            for n in range(2):
                gu[p, h * half:(h + 1) * half, n * ff:(n + 1) * ff] = lax.dot_general(
                    lhs, back[:, n * ff:(n + 1) * ff], (((0,), (0,)), ((), ())),
                    preferred_element_type=f32,
                ).astype(bf16)
        reduce_step(p, True)

    def finish(wide):
        for k in (2, 3, 4, 5):
            reduce_copy(k, wide).wait_recv()

    def total(own, one, two):
        return (own.astype(f32) + one.astype(f32) + two.astype(f32)).astype(bf16)

    finish(False)
    down_out[:fhalf] = total(dn[3, :fhalf], dn_x[1], dn_two[0])
    down_out[fhalf:] = total(dn[3, fhalf:], dn_y[1], dn_two[1])
    for q in range(1, chips):
        zp = other(q)
        remote(
            part.at[zp * 2 + c], far_part.at[zp], part_send.at[q], part_recv.at[zp], "expert",
            zp * 2 + c,
        ).wait_recv()
    mixed = part[me].astype(f32)
    for q in range(1, chips):
        mixed = mixed + far_part[other(q)].astype(f32)
    combined[...] = mixed.astype(bf16)
    finish(True)
    for n, out in ((0, gate_out), (1, up_out)):
        cols = slice(n * ff, (n + 1) * ff)
        out[:half] = total(gu[3, :half, cols], gu_x[1, :, cols], gu_two[0, :, cols])
        out[half:] = total(gu[3, half:, cols], gu_y[1, :, cols], gu_two[1, :, cols])

    each_target(lambda q: tok_copy(q).wait_send())
    for p in range(replicas):
        each_target(lambda q: cot_copy(p, q).wait_send())
    for r in range(1, experts):
        wt_copy(r).wait_send()
    for q in range(chips):
        zp = other(q)
        tok_to_sib(zp).wait_send()
        part_to_sib(zp).wait_send()
        for p in range(replicas):
            cot_to_sib(p, zp).wait_send()
        if q > 0:
            part_copy(q).wait_send()

    @pl.when(inner)
    def _():
        slot = other(last) * 2 + c
        tok_from(slot).wait_send()
        for p in range(replicas):
            cot_from(p, slot).wait_send()

    for wide in (False, True):
        for k in range(6):
            reduce_copy(k, wide).wait_send()


def chain_local(tokens, expert_ids, probs, trade, gate_weight, up_weight, down_weight, out_grad):
    count, width = tokens.shape
    ff = gate_weight.shape[2]
    experts = lax.axis_size("expert")
    replicas = lax.axis_size("dp")
    chips = experts // 2
    share = width // replicas
    halfway = experts // 2
    numbers = jnp.arange(experts, dtype=jnp.int32)
    owners = jnp.where(trade[numbers % halfway] == 1, jnp.bitwise_xor(numbers, halfway), numbers)
    weights = jnp.sum(
        jnp.where(expert_ids.T[None] == owners[:, None, None], probs.T[None], 0.0), axis=1
    )
    bf16, f32 = jnp.bfloat16, jnp.float32
    dma = pltpu.SemaphoreType.DMA
    total = experts * count
    hbm = pl.BlockSpec(memory_space=pl.ANY)
    vmem = pl.BlockSpec(memory_space=pltpu.VMEM)
    combined, gate, up, down = pl.pallas_call(
        layer_kernel,
        out_shape=(
            jax.ShapeDtypeStruct((count, width), bf16),
            jax.ShapeDtypeStruct((share, ff), bf16),
            jax.ShapeDtypeStruct((share, ff), bf16),
            jax.ShapeDtypeStruct((ff, share), bf16),
        ),
        in_specs=[hbm] * 6,
        out_specs=(vmem,) * 4,
        scratch_shapes=[
            pltpu.VMEM((experts, count, width), bf16),
            pltpu.VMEM((replicas, experts, count, share), bf16),
            pltpu.VMEM((experts, experts, count), f32),
            pltpu.VMEM((width, ff), bf16),
            pltpu.VMEM((width, ff), bf16),
            pltpu.VMEM((ff, width), bf16),
            pltpu.VMEM((total, count), f32),
            pltpu.VMEM((total, ff), bf16),
            pltpu.VMEM((total, 2 * ff), bf16),
            pltpu.VMEM((total, ff), f32),
            pltpu.VMEM((total, share), bf16),
            pltpu.VMEM((experts, count, width), bf16),
            pltpu.VMEM((chips, count, width), bf16),
            pltpu.VMEM((chips, count, width), bf16),
            pltpu.VMEM((replicas, share, 2 * ff), bf16),
            pltpu.VMEM((replicas, ff, share), bf16),
            pltpu.VMEM((2, share // 2, 2 * ff), bf16),
            pltpu.VMEM((2, share // 2, 2 * ff), bf16),
            pltpu.VMEM((2, ff // 2, share), bf16),
            pltpu.VMEM((2, ff // 2, share), bf16),
            pltpu.VMEM((2, share // 2, 2 * ff), bf16),
            pltpu.VMEM((2, ff // 2, share), bf16),
            dma((5 + replicas,)),
            dma((chips,)),
            dma((chips,)),
            dma((experts,)),
            dma((replicas, chips)),
            dma((replicas, chips)),
            dma((replicas, experts)),
            dma((experts,)),
            dma((experts,)),
            dma((chips,)),
            dma((chips,)),
            dma((chips,)),
            dma((chips,)),
            dma((12,)),
            dma((12,)),
        ],
        compiler_params=pltpu.CompilerParams(
            collective_id=0, has_side_effects=True, vmem_limit_bytes=67043328
        ),
    )(tokens, out_grad, weights, gate_weight[0], up_weight[0], down_weight[0])
    return combined, gate[None], up[None], down[None]


def local(tokens, expert_ids, *rest):
    experts, replicas = lax.axis_size("expert"), lax.axis_size("dp")
    capacity = 5 * tokens.shape[0] * expert_ids.shape[1] // (4 * experts)
    if tokens.shape[0] <= 2 * capacity and experts == 8 and replicas == 4:
        return chain_local(tokens, expert_ids, *rest)
    return sparse_local(tokens, expert_ids, *rest)


def solution(mesh):
    return jax.shard_map(
        local,
        mesh=mesh,
        in_specs=(
            P(("dp", "expert"), None),
            P(("dp", "expert"), None),
            P(("dp", "expert"), None),
            P(),
            P("expert", None, None),
            P("expert", None, None),
            P("expert", None, None),
            P(("dp", "expert"), None),
        ),
        out_specs=(
            P(("dp", "expert"), None),
            P("expert", "dp", None),
            P("expert", "dp", None),
            P("expert", None, "dp"),
        ),
        check_vma=False,
    )
```

```python
import functools
import jax
import jax.numpy as jnp
from jax import lax
from jax.experimental import pallas as pl
from jax.experimental.pallas import tpu as pltpu
from jax.sharding import PartitionSpec as P


def sparse_local(tokens, expert_ids, probs, trade, gate_weight, up_weight, down_weight, out_grad):
    tok_count, model_width = tokens.shape
    top_count = expert_ids.shape[1]
    hidden_width = gate_weight.shape[2]
    experts = lax.axis_size("expert")
    capacity = 5 * tok_count * top_count // (4 * experts)
    halfway = experts // 2
    chosen = expert_ids.reshape(-1)
    numbers = jnp.arange(experts, dtype=jnp.int32)
    onehot = (chosen[:, None] == numbers[None, :]).astype(jnp.int32)
    earlier = jnp.cumsum(onehot, axis=0) - onehot
    slots = chosen * capacity + jnp.sum(earlier * onehot, axis=1)
    owners = jnp.where(trade[numbers % halfway] == 1, jnp.bitwise_xor(numbers, halfway), numbers)
    pair_tokens = jnp.arange(chosen.shape[0], dtype=jnp.int32) // top_count
    send_rows = (
        jnp.zeros((experts * capacity, model_width), jnp.bfloat16)
        .at[slots]
        .set(tokens[pair_tokens])
    )
    send_rows = send_rows.reshape(experts, capacity, model_width)
    out_pairs = (probs[:, :, None] * out_grad[:, None, :].astype(jnp.float32)).astype(jnp.bfloat16)
    send_grads = (
        jnp.zeros((experts * capacity, model_width), jnp.bfloat16)
        .at[slots]
        .set(out_pairs.reshape(-1, model_width))
    )
    send_grads = send_grads.reshape(experts, capacity, model_width)
    send_rows = send_rows[owners]
    send_grads = send_grads[owners]
    w_gate = gate_weight[0]
    w_up = up_weight[0]
    w_down = down_weight[0]
    arrived = lax.all_to_all(send_rows, "expert", split_axis=0, concat_axis=0, tiled=True)
    lead = arrived.shape[:2]
    flat_rows = arrived.reshape(-1, model_width)
    gate_act = jnp.dot(flat_rows, w_gate, preferred_element_type=jnp.float32)
    up_act = jnp.dot(flat_rows, w_up, preferred_element_type=jnp.float32)
    forward_hidden = (gate_act * jax.nn.sigmoid(gate_act) * up_act).astype(jnp.bfloat16)
    expert_out = jnp.dot(forward_hidden, w_down, preferred_element_type=jnp.float32).astype(
        jnp.bfloat16
    )
    arrived, expert_out, hidden, gate_act, up_act = (
        arrived,
        expert_out.reshape(lead + (model_width,)),
        forward_hidden.reshape(lead + (hidden_width,)),
        gate_act.reshape(lead + (hidden_width,)),
        up_act.reshape(lead + (hidden_width,)),
    )
    returned = lax.all_to_all(expert_out, "expert", split_axis=0, concat_axis=0, tiled=True)
    out_rows = lax.all_to_all(send_grads, "expert", split_axis=0, concat_axis=0, tiled=True)
    returned = returned[owners]
    picked = returned.reshape(-1, model_width)[slots].reshape(tok_count, top_count, model_width)
    combined = jnp.sum(probs[:, :, None] * picked.astype(jnp.float32), axis=1).astype(jnp.bfloat16)
    expert_rows = arrived.reshape(-1, model_width)
    out_rows = out_rows.reshape(-1, model_width)
    hidden = hidden.reshape(-1, hidden_width)
    gate_act = gate_act.reshape(-1, hidden_width)
    up_act = up_act.reshape(-1, hidden_width)
    hidden_grad = lax.dot_general(
        out_rows, w_down, (((1,), (1,)), ((), ())), preferred_element_type=jnp.float32
    )
    sigma = jax.nn.sigmoid(gate_act)
    gate_back = (hidden_grad * up_act * (sigma * (1.0 + gate_act * (1.0 - sigma)))).astype(
        jnp.bfloat16
    )
    up_back = (hidden_grad * (gate_act * sigma)).astype(jnp.bfloat16)
    both_back = jnp.concatenate([gate_back, up_back], axis=1)
    first = lax.dot_general(
        expert_rows, both_back, (((0,), (0,)), ((), ())), preferred_element_type=jnp.float32
    )
    second = lax.dot_general(
        out_rows, hidden, (((0,), (0,)), ((), ())), preferred_element_type=jnp.float32
    )
    summed = lax.psum_scatter(
        jnp.concatenate([first, second], axis=1).astype(jnp.bfloat16),
        "dp",
        scatter_dimension=0,
        tiled=True,
    )
    gate_part = summed[:, :hidden_width]
    up_part = summed[:, hidden_width : 2 * hidden_width]
    down_part = summed[:, 2 * hidden_width :].T
    return (combined, gate_part[None], up_part[None], down_part[None])


def layer_kernel(
    tokens, grads, weights, wg_hbm, wu_hbm, wd_hbm, combined, gate_out, up_out, down_out,
    rows, cots, wts, wg, wu, wd, wcol, hidden, back, acc, pairs, part, sib_part, far_part,
    gu, dn, gu_x, gu_y, dn_x, dn_y, gu_two, dn_two,
    load_sem, tok_send, tok_sib, tok_recv, cot_send, cot_sib, cot_recv, wt_send, wt_recv,
    part_sib, part_sib_recv, part_send, part_recv, red_send, red_recv,
):
    f32 = jnp.float32
    bf16 = jnp.bfloat16
    experts = lax.axis_size("expert")
    chips = experts // 2
    last = chips - 1
    replicas = lax.axis_size("dp")
    count, width = tokens.shape
    share = width // replicas
    ff = wg.shape[1]
    me = lax.axis_index("expert")
    z = me // 2
    c = me % 2
    d = lax.axis_index("dp")
    dx = (d // 2) * 2 + (1 - d % 2)
    dy = (1 - d // 2) * 2 + d % 2
    dd = 3 - d
    upper = z // (chips // 2)
    zm = z * (1 - upper) + (last - z) * upper
    sibling = z * 2 + (1 - c)
    inner = zm == 1

    def at_chip(m):
        return m * (1 - upper) + (last - m) * upper

    def other(q):
        return at_chip(jnp.where(q == 0, zm, jnp.where(q == 1, 1 - zm, q)))

    def source(q):
        m = jnp.where(jnp.logical_and(inner, q >= 2), last + 2 - q, q)
        return at_chip(jnp.where(q == 0, zm, jnp.where(q == 1, 1 - zm, m)))

    def owner_of(p):
        return jnp.where(p == 0, dd, jnp.where(p == 1, dx, jnp.where(p == 2, dy, d)))

    def lanes(p):
        return pl.ds(pl.multiple_of(owner_of(p) * share, share), share)

    def remote(src, dst, ssem, rsem, axis, to):
        return pltpu.make_async_remote_copy(
            src_ref=src, dst_ref=dst, send_sem=ssem, recv_sem=rsem,
            device_id={axis: to}, device_id_type=pl.DeviceIdType.MESH,
        )

    loads = [
        pltpu.make_async_copy(wg_hbm, wg, load_sem.at[0]),
        pltpu.make_async_copy(wu_hbm, wu, load_sem.at[1]),
        pltpu.make_async_copy(wd_hbm, wd, load_sem.at[2]),
        pltpu.make_async_copy(tokens, rows.at[me], load_sem.at[3]),
        pltpu.make_async_copy(weights, wts.at[me], load_sem.at[4]),
    ]
    loads[3].start()
    loads[4].start()

    def cot_load(p):
        return pltpu.make_async_copy(grads.at[:, lanes(p)], cots.at[p, me], load_sem.at[5 + p])

    for load in loads[:3]:
        load.start()
    for p in range(replicas):
        cot_load(p).start()

    barrier = pltpu.get_barrier_semaphore()
    for r in range(1, experts):
        pl.semaphore_signal(
            barrier, inc=1, device_id={"expert": (me + r) % experts},
            device_id_type=pl.DeviceIdType.MESH,
        )
    for to in (dx, dy):
        pl.semaphore_signal(
            barrier, inc=1, device_id={"dp": to}, device_id_type=pl.DeviceIdType.MESH
        )
    pl.semaphore_wait(barrier, experts + 1)

    def tok_copy(q):
        to = other(q) * 2 + c
        return remote(tokens, rows.at[me], tok_send.at[q], tok_recv.at[me], "expert", to)

    def cot_copy(p, q):
        to = other(q) * 2 + c
        return remote(
            grads.at[:, lanes(p)], cots.at[p, me], cot_send.at[p, q], cot_recv.at[p, me],
            "expert", to,
        )

    def each_target(fn):
        for q in range(1, chips):
            if q < last:
                fn(q)
            else:
                pl.when(inner)(functools.partial(fn, q))

    def wt_copy(r):
        return remote(
            weights, wts.at[me], wt_send.at[r], wt_recv.at[me], "expert", (me + r) % experts
        )

    for r in range(1, experts):
        wt_copy(r).start()
    each_target(lambda q: tok_copy(q).start())

    end = at_chip(0) * 2 + c

    def tok_from(slot):
        return remote(rows.at[slot], rows.at[slot], tok_send.at[0], tok_recv.at[slot], "expert", end)

    def tok_to_sib(zp):
        slot = zp * 2 + c
        return remote(
            rows.at[slot], rows.at[slot], tok_sib.at[zp], tok_recv.at[slot], "expert", sibling
        )

    def cot_from(p, slot):
        ref = cots.at[p, slot]
        return remote(ref, ref, cot_send.at[p, 0], cot_recv.at[p, slot], "expert", end)

    def cot_to_sib(p, zp):
        slot = zp * 2 + c
        ref = cots.at[p, slot]
        return remote(ref, ref, cot_sib.at[p, zp], cot_recv.at[p, slot], "expert", sibling)

    def part_to_sib(zp):
        return remote(
            part.at[zp * 2 + (1 - c)], sib_part.at[zp], part_sib.at[zp], part_sib_recv.at[zp],
            "expert", sibling,
        )

    loads[4].wait()
    for r in range(1, experts):
        slot = (me + r) % experts
        remote(weights, wts.at[slot], wt_send.at[r], wt_recv.at[slot], "expert", slot).wait_recv()
    eye = lax.broadcasted_iota(jnp.int32, (count, count), 0) == lax.broadcasted_iota(
        jnp.int32, (count, count), 1
    )
    for slot in range(experts):
        row = jnp.broadcast_to(wts[slot, pl.ds(me, 1), :], (count, count))
        column = jnp.sum(jnp.where(eye, row, 0.0), axis=1, keepdims=True)
        wcol[pl.ds(slot * count, count), :] = jnp.broadcast_to(column, (count, wcol.shape[1]))

    pair = 2 * count

    @pl.loop(0, chips)
    def _(q):
        zp = source(q)

        @pl.when(q == last)
        def _():
            for p in range(2):
                each_target(lambda q: cot_copy(p, q).start())

        @pl.when(q == 0)
        def _():
            loads[3].wait()

        @pl.when(q > 0)
        def _():
            tok_from(zp * 2 + c).wait_recv()

        @pl.when(jnp.logical_and(inner, q == last - 1))
        def _():
            tok_from(zp * 2 + c).start()

        tok_to_sib(zp).start()

        @pl.when(q == 0)
        def _():
            for load in loads[:3]:
                load.wait()

        tok_from(zp * 2 + (1 - c)).wait_recv()
        where = pl.ds(pl.multiple_of(zp * pair, pair), pair)
        x = rows[pl.ds(zp * 2, 2)].reshape(pair, width)
        tile = ff // 3

        @pl.loop(0, 3)
        def _(n):
            cols = pl.ds(pl.multiple_of(n * tile, tile), tile)
            g = jnp.dot(x, wg[:, cols], preferred_element_type=f32)
            u = jnp.dot(x, wu[:, cols], preferred_element_type=f32)
            sigma = jax.nn.sigmoid(g)
            silu = g * sigma
            hidden[where, cols] = (silu * u).astype(bf16)
            back[where, cols] = (u * (sigma * (1.0 + g * (1.0 - sigma)))).astype(bf16)
            back[where, pl.ds(pl.multiple_of(ff + n * tile, tile), tile)] = silu.astype(bf16)

        @pl.loop(0, replicas)
        def _(n):
            cols = pl.ds(pl.multiple_of(n * share, share), share)
            o = jnp.dot(hidden[where, :], wd[:, cols], preferred_element_type=f32)
            o = (o * wcol[where, 0:1]).astype(bf16)
            part[zp * 2, :, cols] = o[:count]
            part[zp * 2 + 1, :, cols] = o[count:]

        part_to_sib(zp).start()

    def part_copy(q):
        zp = other(q)
        return remote(
            part.at[zp * 2 + c], far_part.at[z], part_send.at[q], part_recv.at[z], "expert",
            zp * 2 + c,
        )

    half = share // 2
    fhalf = ff // 2

    def reduce_copy(step, wide):
        send, far = (gu, (gu_x, gu_y, gu_two)) if wide else (dn, (dn_x, dn_y, dn_two))
        h = half if wide else fhalf
        lo, hi = pl.ds(0, h), pl.ds(h, h)
        src, dst, axis_to = {
            0: (send.at[0, lo], far[0].at[0], dx),
            1: (send.at[0, hi], far[1].at[0], dy),
            2: (send.at[1, lo], far[0].at[1], dx),
            3: (send.at[2, hi], far[1].at[1], dy),
            4: (send.at[2, lo], far[2].at[0], dy),
            5: (send.at[1, hi], far[2].at[1], dx),
        }[step]
        k = step + 6 * int(wide)
        return remote(src, dst, red_send.at[k], red_recv.at[k], "dp", axis_to)

    def reduce_step(p, wide):
        send, far = (gu, (gu_x, gu_y)) if wide else (dn, (dn_x, dn_y))
        h = half if wide else fhalf
        lo, hi = pl.ds(0, h), pl.ds(h, h)

        @pl.when(p == 0)
        def _():
            reduce_copy(0, wide).start()
            reduce_copy(1, wide).start()

        @pl.when(p == 1)
        def _():
            reduce_copy(2, wide).start()

        @pl.when(p == 2)
        def _():
            reduce_copy(3, wide).start()

        @pl.when(p == (3 if wide else 2))
        def _():
            reduce_copy(0, wide).wait_recv()
            send[2, lo] = (send[2, lo].astype(f32) + far[0][0].astype(f32)).astype(bf16)
            reduce_copy(4, wide).start()
            reduce_copy(1, wide).wait_recv()
            send[1, hi] = (send[1, hi].astype(f32) + far[1][0].astype(f32)).astype(bf16)
            reduce_copy(5, wide).start()

    @pl.loop(0, replicas)
    def _(p):
        for q in range(chips):
            zp = source(q)
            if q == 0:
                cot_load(p).wait()
            else:
                cot_from(p, zp * 2 + c).wait_recv()
            if q == last - 1:

                @pl.when(inner)
                def _():
                    cot_from(p, zp * 2 + c).start()

            cot_to_sib(p, zp).start()

        @pl.when(p < replicas - 2)
        def _():
            each_target(lambda q: cot_copy(p + 2, q).start())

        @pl.when(p == replicas - 1)
        def _():
            for q in range(last, 0, -1):
                part_copy(q).start()

        for zp in range(chips):
            cot_from(p, zp * 2 + (1 - c)).wait_recv()
        for slot in range(experts):
            where = pl.ds(slot * count, count)
            pairs[where, :] = (wcol[where, 0:1] * cots[p, slot].astype(f32)).astype(bf16)
        tile = ff // 3

        @pl.loop(0, 3)
        def _(n):
            cols = pl.ds(pl.multiple_of(n * tile, tile), tile)
            dn[p, cols, :] = lax.dot_general(
                hidden[:, cols], pairs[...], (((0,), (0,)), ((), ())), preferred_element_type=f32
            ).astype(bf16)

        reduce_step(p, False)

        @pl.when(p == 0)
        def _():
            for zp in range(chips):
                remote(
                    part.at[zp * 2 + (1 - c)], sib_part.at[zp], part_sib.at[zp],
                    part_sib_recv.at[zp], "expert", sibling,
                ).wait_recv()
                part[zp * 2 + c] = (
                    part[zp * 2 + c].astype(f32) + sib_part[zp].astype(f32)
                ).astype(bf16)

        @pl.loop(0, 3)
        def _(n):
            cols = pl.ds(pl.multiple_of(n * tile, tile), tile)
            more = lax.dot_general(
                pairs[...], wd[cols, lanes(p)], (((1,), (1,)), ((), ())),
                preferred_element_type=f32,
            )
            acc[:, cols] = jnp.where(p == 0, more, acc[:, cols] + more)

    @pl.loop(0, experts)
    def _(n):
        where = pl.ds(pl.multiple_of(n * count, count), count)
        back[where, :ff] = (acc[where, :] * back[where, :ff].astype(f32)).astype(bf16)
        back[where, ff:] = (acc[where, :] * back[where, ff:].astype(f32)).astype(bf16)

    @pl.loop(0, replicas)
    def _(p):
        for h in range(2):
            cols = pl.ds(pl.multiple_of(owner_of(p) * share + h * half, half), half)
            lhs = rows[:, :, cols].reshape(experts * count, half)
            for n in range(2):
                gu[p, h * half:(h + 1) * half, n * ff:(n + 1) * ff] = lax.dot_general(
                    lhs, back[:, n * ff:(n + 1) * ff], (((0,), (0,)), ((), ())),
                    preferred_element_type=f32,
                ).astype(bf16)
        reduce_step(p, True)

    def finish(wide):
        for k in (2, 3, 4, 5):
            reduce_copy(k, wide).wait_recv()

    def total(own, one, two):
        return (own.astype(f32) + one.astype(f32) + two.astype(f32)).astype(bf16)

    finish(False)
    down_out[:fhalf] = total(dn[3, :fhalf], dn_x[1], dn_two[0])
    down_out[fhalf:] = total(dn[3, fhalf:], dn_y[1], dn_two[1])
    for q in range(1, chips):
        zp = other(q)
        remote(
            part.at[zp * 2 + c], far_part.at[zp], part_send.at[q], part_recv.at[zp], "expert",
            zp * 2 + c,
        ).wait_recv()
    mixed = part[me].astype(f32)
    for q in range(1, chips):
        mixed = mixed + far_part[other(q)].astype(f32)
    combined[...] = mixed.astype(bf16)
    finish(True)
    for n, out in ((0, gate_out), (1, up_out)):
        cols = slice(n * ff, (n + 1) * ff)
        out[:half] = total(gu[3, :half, cols], gu_x[1, :, cols], gu_two[0, :, cols])
        out[half:] = total(gu[3, half:, cols], gu_y[1, :, cols], gu_two[1, :, cols])

    each_target(lambda q: tok_copy(q).wait_send())
    for p in range(replicas):
        each_target(lambda q: cot_copy(p, q).wait_send())
    for r in range(1, experts):
        wt_copy(r).wait_send()
    for q in range(chips):
        zp = other(q)
        tok_to_sib(zp).wait_send()
        part_to_sib(zp).wait_send()
        for p in range(replicas):
            cot_to_sib(p, zp).wait_send()
        if q > 0:
            part_copy(q).wait_send()

    @pl.when(inner)
    def _():
        slot = source(last - 1) * 2 + c
        tok_from(slot).wait_send()
        for p in range(replicas):
            cot_from(p, slot).wait_send()

    for wide in (False, True):
        for k in range(6):
            reduce_copy(k, wide).wait_send()


def chain_local(tokens, expert_ids, probs, trade, gate_weight, up_weight, down_weight, out_grad):
    count, width = tokens.shape
    ff = gate_weight.shape[2]
    experts = lax.axis_size("expert")
    replicas = lax.axis_size("dp")
    chips = experts // 2
    share = width // replicas
    halfway = experts // 2
    numbers = jnp.arange(experts, dtype=jnp.int32)
    owners = jnp.where(
        jnp.concatenate([trade, trade]) == 1, jnp.bitwise_xor(numbers, halfway), numbers
    )
    weights = jnp.sum(
        jnp.where(expert_ids.T[None] == owners[:, None, None], probs.T[None], 0.0), axis=1
    )
    bf16, f32 = jnp.bfloat16, jnp.float32
    dma = pltpu.SemaphoreType.DMA
    total = experts * count
    hbm = pl.BlockSpec(memory_space=pl.ANY)
    vmem = pl.BlockSpec(memory_space=pltpu.VMEM)
    combined, gate, up, down = pl.pallas_call(
        layer_kernel,
        out_shape=(
            jax.ShapeDtypeStruct((count, width), bf16),
            jax.ShapeDtypeStruct((share, ff), bf16),
            jax.ShapeDtypeStruct((share, ff), bf16),
            jax.ShapeDtypeStruct((ff, share), bf16),
        ),
        in_specs=[hbm] * 6,
        out_specs=(vmem,) * 4,
        scratch_shapes=[
            pltpu.VMEM((experts, count, width), bf16),
            pltpu.VMEM((replicas, experts, count, share), bf16),
            pltpu.VMEM((experts, experts, count), f32),
            pltpu.VMEM((width, ff), bf16),
            pltpu.VMEM((width, ff), bf16),
            pltpu.VMEM((ff, width), bf16),
            pltpu.VMEM((total, count), f32),
            pltpu.VMEM((total, ff), bf16),
            pltpu.VMEM((total, 2 * ff), bf16),
            pltpu.VMEM((total, ff), f32),
            pltpu.VMEM((total, share), bf16),
            pltpu.VMEM((experts, count, width), bf16),
            pltpu.VMEM((chips, count, width), bf16),
            pltpu.VMEM((chips, count, width), bf16),
            pltpu.VMEM((replicas, share, 2 * ff), bf16),
            pltpu.VMEM((replicas, ff, share), bf16),
            pltpu.VMEM((2, share // 2, 2 * ff), bf16),
            pltpu.VMEM((2, share // 2, 2 * ff), bf16),
            pltpu.VMEM((2, ff // 2, share), bf16),
            pltpu.VMEM((2, ff // 2, share), bf16),
            pltpu.VMEM((2, share // 2, 2 * ff), bf16),
            pltpu.VMEM((2, ff // 2, share), bf16),
            dma((5 + replicas,)),
            dma((chips,)),
            dma((chips,)),
            dma((experts,)),
            dma((replicas, chips)),
            dma((replicas, chips)),
            dma((replicas, experts)),
            dma((experts,)),
            dma((experts,)),
            dma((chips,)),
            dma((chips,)),
            dma((chips,)),
            dma((chips,)),
            dma((12,)),
            dma((12,)),
        ],
        compiler_params=pltpu.CompilerParams(
            collective_id=0, has_side_effects=True, vmem_limit_bytes=67043328
        ),
    )(tokens, out_grad, weights, gate_weight[0], up_weight[0], down_weight[0])
    return combined, gate[None], up[None], down[None]


def local(tokens, expert_ids, *rest):
    experts, replicas = lax.axis_size("expert"), lax.axis_size("dp")
    capacity = 5 * tokens.shape[0] * expert_ids.shape[1] // (4 * experts)
    if tokens.shape[0] <= 2 * capacity and experts == 8 and replicas == 4:
        return chain_local(tokens, expert_ids, *rest)
    return sparse_local(tokens, expert_ids, *rest)


def solution(mesh):
    return jax.shard_map(
        local,
        mesh=mesh,
        in_specs=(
            P(("dp", "expert"), None),
            P(("dp", "expert"), None),
            P(("dp", "expert"), None),
            P(),
            P("expert", None, None),
            P("expert", None, None),
            P("expert", None, None),
            P(("dp", "expert"), None),
        ),
        out_specs=(
            P(("dp", "expert"), None),
            P("expert", "dp", None),
            P("expert", "dp", None),
            P("expert", None, "dp"),
        ),
        check_vma=False,
    )
```

```python
import functools
import jax
import jax.numpy as jnp
from jax import lax
from jax.experimental import pallas as pl
from jax.experimental.pallas import tpu as pltpu
from jax.sharding import PartitionSpec as P


def sparse_local(tokens, expert_ids, probs, trade, gate_weight, up_weight, down_weight, out_grad):
    tok_count, model_width = tokens.shape
    top_count = expert_ids.shape[1]
    hidden_width = gate_weight.shape[2]
    experts = lax.axis_size("expert")
    capacity = 5 * tok_count * top_count // (4 * experts)
    halfway = experts // 2
    chosen = expert_ids.reshape(-1)
    numbers = jnp.arange(experts, dtype=jnp.int32)
    onehot = (chosen[:, None] == numbers[None, :]).astype(jnp.int32)
    earlier = jnp.cumsum(onehot, axis=0) - onehot
    slots = chosen * capacity + jnp.sum(earlier * onehot, axis=1)
    owners = jnp.where(trade[numbers % halfway] == 1, jnp.bitwise_xor(numbers, halfway), numbers)
    pair_tokens = jnp.arange(chosen.shape[0], dtype=jnp.int32) // top_count
    send_rows = (
        jnp.zeros((experts * capacity, model_width), jnp.bfloat16)
        .at[slots]
        .set(tokens[pair_tokens])
    )
    send_rows = send_rows.reshape(experts, capacity, model_width)
    out_pairs = (probs[:, :, None] * out_grad[:, None, :].astype(jnp.float32)).astype(jnp.bfloat16)
    send_grads = (
        jnp.zeros((experts * capacity, model_width), jnp.bfloat16)
        .at[slots]
        .set(out_pairs.reshape(-1, model_width))
    )
    send_grads = send_grads.reshape(experts, capacity, model_width)
    send_rows = send_rows[owners]
    send_grads = send_grads[owners]
    w_gate = gate_weight[0]
    w_up = up_weight[0]
    w_down = down_weight[0]
    arrived = lax.all_to_all(send_rows, "expert", split_axis=0, concat_axis=0, tiled=True)
    lead = arrived.shape[:2]
    flat_rows = arrived.reshape(-1, model_width)
    gate_act = jnp.dot(flat_rows, w_gate, preferred_element_type=jnp.float32)
    up_act = jnp.dot(flat_rows, w_up, preferred_element_type=jnp.float32)
    forward_hidden = (gate_act * jax.nn.sigmoid(gate_act) * up_act).astype(jnp.bfloat16)
    expert_out = jnp.dot(forward_hidden, w_down, preferred_element_type=jnp.float32).astype(
        jnp.bfloat16
    )
    arrived, expert_out, hidden, gate_act, up_act = (
        arrived,
        expert_out.reshape(lead + (model_width,)),
        forward_hidden.reshape(lead + (hidden_width,)),
        gate_act.reshape(lead + (hidden_width,)),
        up_act.reshape(lead + (hidden_width,)),
    )
    returned = lax.all_to_all(expert_out, "expert", split_axis=0, concat_axis=0, tiled=True)
    out_rows = lax.all_to_all(send_grads, "expert", split_axis=0, concat_axis=0, tiled=True)
    returned = returned[owners]
    picked = returned.reshape(-1, model_width)[slots].reshape(tok_count, top_count, model_width)
    combined = jnp.sum(probs[:, :, None] * picked.astype(jnp.float32), axis=1).astype(jnp.bfloat16)
    expert_rows = arrived.reshape(-1, model_width)
    out_rows = out_rows.reshape(-1, model_width)
    hidden = hidden.reshape(-1, hidden_width)
    gate_act = gate_act.reshape(-1, hidden_width)
    up_act = up_act.reshape(-1, hidden_width)
    hidden_grad = lax.dot_general(
        out_rows, w_down, (((1,), (1,)), ((), ())), preferred_element_type=jnp.float32
    )
    sigma = jax.nn.sigmoid(gate_act)
    gate_back = (hidden_grad * up_act * (sigma * (1.0 + gate_act * (1.0 - sigma)))).astype(
        jnp.bfloat16
    )
    up_back = (hidden_grad * (gate_act * sigma)).astype(jnp.bfloat16)
    both_back = jnp.concatenate([gate_back, up_back], axis=1)
    first = lax.dot_general(
        expert_rows, both_back, (((0,), (0,)), ((), ())), preferred_element_type=jnp.float32
    )
    second = lax.dot_general(
        out_rows, hidden, (((0,), (0,)), ((), ())), preferred_element_type=jnp.float32
    )
    summed = lax.psum_scatter(
        jnp.concatenate([first, second], axis=1).astype(jnp.bfloat16),
        "dp",
        scatter_dimension=0,
        tiled=True,
    )
    gate_part = summed[:, :hidden_width]
    up_part = summed[:, hidden_width : 2 * hidden_width]
    down_part = summed[:, 2 * hidden_width :].T
    return (combined, gate_part[None], up_part[None], down_part[None])


def layer_kernel(
    tokens, grads, weights, wg_hbm, wu_hbm, wd_hbm, combined, gate_out, up_out, down_out,
    rows, cots, wts, wg, wu, wd, wcol, hidden, back, acc, pairs, part, sib_part, far_part,
    gu, dn, gu_x, gu_y, dn_x, dn_y, gu_two, dn_two,
    load_sem, tok_send, tok_sib, tok_recv, cot_send, cot_sib, cot_recv, wt_send, wt_recv,
    part_sib, part_sib_recv, part_send, part_recv, red_send, red_recv,
):
    f32 = jnp.float32
    bf16 = jnp.bfloat16
    experts = lax.axis_size("expert")
    chips = experts // 2
    last = chips - 1
    replicas = lax.axis_size("dp")
    count, width = tokens.shape
    share = width // replicas
    ff = wg.shape[1]
    me = lax.axis_index("expert")
    z = me // 2
    c = me % 2
    d = lax.axis_index("dp")
    dx = (d // 2) * 2 + (1 - d % 2)
    dy = (1 - d // 2) * 2 + d % 2
    dd = 3 - d
    upper = z // (chips // 2)
    zm = z * (1 - upper) + (last - z) * upper
    sibling = z * 2 + (1 - c)
    inner = zm == 1

    def at_chip(m):
        return m * (1 - upper) + (last - m) * upper

    def other(q):
        return at_chip(jnp.where(q == 0, zm, jnp.where(q == 1, 1 - zm, q)))

    def source(q):
        m = jnp.where(jnp.logical_and(inner, q >= 2), last + 2 - q, q)
        return at_chip(jnp.where(q == 0, zm, jnp.where(q == 1, 1 - zm, m)))

    def owner_of(p):
        return jnp.where(p == 0, dd, jnp.where(p == 1, dx, jnp.where(p == 2, dy, d)))

    def lanes(p):
        return pl.ds(pl.multiple_of(owner_of(p) * share, share), share)

    def remote(src, dst, ssem, rsem, axis, to):
        return pltpu.make_async_remote_copy(
            src_ref=src, dst_ref=dst, send_sem=ssem, recv_sem=rsem,
            device_id={axis: to}, device_id_type=pl.DeviceIdType.MESH,
        )

    loads = [
        pltpu.make_async_copy(wg_hbm, wg, load_sem.at[0]),
        pltpu.make_async_copy(wu_hbm, wu, load_sem.at[1]),
        pltpu.make_async_copy(wd_hbm, wd, load_sem.at[2]),
        pltpu.make_async_copy(tokens, rows.at[me], load_sem.at[3]),
        pltpu.make_async_copy(weights, wts.at[me], load_sem.at[4]),
    ]
    loads[3].start()
    loads[4].start()

    def cot_load(p):
        return pltpu.make_async_copy(grads.at[:, lanes(p)], cots.at[p, me], load_sem.at[5 + p])

    for load in loads[:3]:
        load.start()
    for p in range(replicas):
        cot_load(p).start()

    barrier = pltpu.get_barrier_semaphore()
    for r in range(1, experts):
        pl.semaphore_signal(
            barrier, inc=1, device_id={"expert": (me + r) % experts},
            device_id_type=pl.DeviceIdType.MESH,
        )
    for to in (dx, dy):
        pl.semaphore_signal(
            barrier, inc=1, device_id={"dp": to}, device_id_type=pl.DeviceIdType.MESH
        )
    pl.semaphore_wait(barrier, experts + 1)

    def tok_copy(q):
        to = other(q) * 2 + c
        return remote(tokens, rows.at[me], tok_send.at[q], tok_recv.at[me], "expert", to)

    def cot_copy(p, q):
        to = other(q) * 2 + c
        return remote(
            grads.at[:, lanes(p)], cots.at[p, me], cot_send.at[p, q], cot_recv.at[p, me],
            "expert", to,
        )

    def each_target(fn):
        for q in (2, 1) + tuple(range(3, chips)):
            if q < last:
                fn(q)
            else:
                pl.when(inner)(functools.partial(fn, q))

    def wt_copy(r):
        return remote(
            weights, wts.at[me], wt_send.at[r], wt_recv.at[me], "expert", (me + r) % experts
        )

    for r in range(1, experts):
        wt_copy(r).start()
    each_target(lambda q: tok_copy(q).start())

    end = at_chip(0) * 2 + c

    def tok_from(slot):
        return remote(rows.at[slot], rows.at[slot], tok_send.at[0], tok_recv.at[slot], "expert", end)

    def tok_to_sib(zp):
        slot = zp * 2 + c
        return remote(
            rows.at[slot], rows.at[slot], tok_sib.at[zp], tok_recv.at[slot], "expert", sibling
        )

    def cot_from(p, slot):
        ref = cots.at[p, slot]
        return remote(ref, ref, cot_send.at[p, 0], cot_recv.at[p, slot], "expert", end)

    def cot_to_sib(p, zp):
        slot = zp * 2 + c
        ref = cots.at[p, slot]
        return remote(ref, ref, cot_sib.at[p, zp], cot_recv.at[p, slot], "expert", sibling)

    def part_to_sib(zp):
        return remote(
            part.at[zp * 2 + (1 - c)], sib_part.at[zp], part_sib.at[zp], part_sib_recv.at[zp],
            "expert", sibling,
        )

    loads[4].wait()
    for r in range(1, experts):
        slot = (me + r) % experts
        remote(weights, wts.at[slot], wt_send.at[r], wt_recv.at[slot], "expert", slot).wait_recv()
    eye = lax.broadcasted_iota(jnp.int32, (count, count), 0) == lax.broadcasted_iota(
        jnp.int32, (count, count), 1
    )
    for slot in range(experts):
        row = jnp.broadcast_to(wts[slot, pl.ds(me, 1), :], (count, count))
        column = jnp.sum(jnp.where(eye, row, 0.0), axis=1, keepdims=True)
        wcol[pl.ds(slot * count, count), :] = jnp.broadcast_to(column, (count, wcol.shape[1]))

    pair = 2 * count

    @pl.loop(0, chips)
    def _(q):
        zp = source(q)

        @pl.when(q == last)
        def _():
            for p in range(2):
                each_target(lambda q: cot_copy(p, q).start())

        @pl.when(q == 0)
        def _():
            loads[3].wait()

        @pl.when(q > 0)
        def _():
            tok_from(zp * 2 + c).wait_recv()

        @pl.when(jnp.logical_and(inner, q == last - 1))
        def _():
            tok_from(zp * 2 + c).start()

        tok_to_sib(zp).start()

        @pl.when(q == 0)
        def _():
            for load in loads[:3]:
                load.wait()

        tok_from(zp * 2 + (1 - c)).wait_recv()
        where = pl.ds(pl.multiple_of(zp * pair, pair), pair)
        x = rows[pl.ds(zp * 2, 2)].reshape(pair, width)
        tile = ff // 3

        @pl.loop(0, 3)
        def _(n):
            cols = pl.ds(pl.multiple_of(n * tile, tile), tile)
            g = jnp.dot(x, wg[:, cols], preferred_element_type=f32)
            u = jnp.dot(x, wu[:, cols], preferred_element_type=f32)
            sigma = jax.nn.sigmoid(g)
            silu = g * sigma
            hidden[where, cols] = (silu * u).astype(bf16)
            back[where, cols] = (u * (sigma * (1.0 + g * (1.0 - sigma)))).astype(bf16)
            back[where, pl.ds(pl.multiple_of(ff + n * tile, tile), tile)] = silu.astype(bf16)

        @pl.loop(0, replicas)
        def _(n):
            cols = pl.ds(pl.multiple_of(n * share, share), share)
            o = jnp.dot(hidden[where, :], wd[:, cols], preferred_element_type=f32)
            o = (o * wcol[where, 0:1]).astype(bf16)
            part[zp * 2, :, cols] = o[:count]
            part[zp * 2 + 1, :, cols] = o[count:]

        part_to_sib(zp).start()

    def part_copy(q):
        zp = other(q)
        return remote(
            part.at[zp * 2 + c], far_part.at[z], part_send.at[q], part_recv.at[z], "expert",
            zp * 2 + c,
        )

    half = share // 2
    fhalf = ff // 2

    def reduce_copy(step, wide):
        send, far = (gu, (gu_x, gu_y, gu_two)) if wide else (dn, (dn_x, dn_y, dn_two))
        h = half if wide else fhalf
        lo, hi = pl.ds(0, h), pl.ds(h, h)
        src, dst, axis_to = {
            0: (send.at[0, lo], far[0].at[0], dx),
            1: (send.at[0, hi], far[1].at[0], dy),
            2: (send.at[1, lo], far[0].at[1], dx),
            3: (send.at[2, hi], far[1].at[1], dy),
            4: (send.at[2, lo], far[2].at[0], dy),
            5: (send.at[1, hi], far[2].at[1], dx),
        }[step]
        k = step + 6 * int(wide)
        return remote(src, dst, red_send.at[k], red_recv.at[k], "dp", axis_to)

    def reduce_step(p, wide):
        send, far = (gu, (gu_x, gu_y)) if wide else (dn, (dn_x, dn_y))
        h = half if wide else fhalf
        lo, hi = pl.ds(0, h), pl.ds(h, h)

        @pl.when(p == 0)
        def _():
            reduce_copy(0, wide).start()
            reduce_copy(1, wide).start()

        @pl.when(p == 1)
        def _():
            reduce_copy(2, wide).start()

        @pl.when(p == 2)
        def _():
            reduce_copy(3, wide).start()

        @pl.when(p == (3 if wide else 2))
        def _():
            reduce_copy(0, wide).wait_recv()
            send[2, lo] = (send[2, lo].astype(f32) + far[0][0].astype(f32)).astype(bf16)
            reduce_copy(4, wide).start()
            reduce_copy(1, wide).wait_recv()
            send[1, hi] = (send[1, hi].astype(f32) + far[1][0].astype(f32)).astype(bf16)
            reduce_copy(5, wide).start()

    @pl.loop(0, replicas)
    def _(p):
        for q in range(chips):
            zp = source(q)
            if q == 0:
                cot_load(p).wait()
            else:
                cot_from(p, zp * 2 + c).wait_recv()
            if q == last - 1:

                @pl.when(inner)
                def _():
                    cot_from(p, zp * 2 + c).start()

            cot_to_sib(p, zp).start()

        @pl.when(p < replicas - 2)
        def _():
            each_target(lambda q: cot_copy(p + 2, q).start())

        @pl.when(p == replicas - 1)
        def _():
            for q in range(last, 0, -1):
                part_copy(q).start()

        for zp in range(chips):
            cot_from(p, zp * 2 + (1 - c)).wait_recv()
        for slot in range(experts):
            where = pl.ds(slot * count, count)
            pairs[where, :] = (wcol[where, 0:1] * cots[p, slot].astype(f32)).astype(bf16)
        tile = ff // 3

        @pl.loop(0, 3)
        def _(n):
            cols = pl.ds(pl.multiple_of(n * tile, tile), tile)
            dn[p, cols, :] = lax.dot_general(
                hidden[:, cols], pairs[...], (((0,), (0,)), ((), ())), preferred_element_type=f32
            ).astype(bf16)

        reduce_step(p, False)

        @pl.when(p == 0)
        def _():
            for zp in range(chips):
                remote(
                    part.at[zp * 2 + (1 - c)], sib_part.at[zp], part_sib.at[zp],
                    part_sib_recv.at[zp], "expert", sibling,
                ).wait_recv()
                part[zp * 2 + c] = (
                    part[zp * 2 + c].astype(f32) + sib_part[zp].astype(f32)
                ).astype(bf16)

        @pl.loop(0, 3)
        def _(n):
            cols = pl.ds(pl.multiple_of(n * tile, tile), tile)
            more = lax.dot_general(
                pairs[...], wd[cols, lanes(p)], (((1,), (1,)), ((), ())),
                preferred_element_type=f32,
            )
            acc[:, cols] = jnp.where(p == 0, more, acc[:, cols] + more)

    @pl.loop(0, experts)
    def _(n):
        where = pl.ds(pl.multiple_of(n * count, count), count)
        back[where, :ff] = (acc[where, :] * back[where, :ff].astype(f32)).astype(bf16)
        back[where, ff:] = (acc[where, :] * back[where, ff:].astype(f32)).astype(bf16)

    @pl.loop(0, replicas)
    def _(p):
        for h in range(2):
            cols = pl.ds(pl.multiple_of(owner_of(p) * share + h * half, half), half)
            lhs = rows[:, :, cols].reshape(experts * count, half)
            for n in range(2):
                gu[p, h * half:(h + 1) * half, n * ff:(n + 1) * ff] = lax.dot_general(
                    lhs, back[:, n * ff:(n + 1) * ff], (((0,), (0,)), ((), ())),
                    preferred_element_type=f32,
                ).astype(bf16)
        reduce_step(p, True)

    def finish(wide):
        for k in (2, 3, 4, 5):
            reduce_copy(k, wide).wait_recv()

    def total(own, one, two):
        return (own.astype(f32) + one.astype(f32) + two.astype(f32)).astype(bf16)

    finish(False)
    down_out[:fhalf] = total(dn[3, :fhalf], dn_x[1], dn_two[0])
    down_out[fhalf:] = total(dn[3, fhalf:], dn_y[1], dn_two[1])
    for q in range(1, chips):
        zp = other(q)
        remote(
            part.at[zp * 2 + c], far_part.at[zp], part_send.at[q], part_recv.at[zp], "expert",
            zp * 2 + c,
        ).wait_recv()
    mixed = part[me].astype(f32)
    for q in range(1, chips):
        mixed = mixed + far_part[other(q)].astype(f32)
    combined[...] = mixed.astype(bf16)
    finish(True)
    for n, out in ((0, gate_out), (1, up_out)):
        cols = slice(n * ff, (n + 1) * ff)
        out[:half] = total(gu[3, :half, cols], gu_x[1, :, cols], gu_two[0, :, cols])
        out[half:] = total(gu[3, half:, cols], gu_y[1, :, cols], gu_two[1, :, cols])

    each_target(lambda q: tok_copy(q).wait_send())
    for p in range(replicas):
        each_target(lambda q: cot_copy(p, q).wait_send())
    for r in range(1, experts):
        wt_copy(r).wait_send()
    for q in range(chips):
        zp = other(q)
        tok_to_sib(zp).wait_send()
        part_to_sib(zp).wait_send()
        for p in range(replicas):
            cot_to_sib(p, zp).wait_send()
        if q > 0:
            part_copy(q).wait_send()

    @pl.when(inner)
    def _():
        slot = source(last - 1) * 2 + c
        tok_from(slot).wait_send()
        for p in range(replicas):
            cot_from(p, slot).wait_send()

    for wide in (False, True):
        for k in range(6):
            reduce_copy(k, wide).wait_send()


def chain_local(tokens, expert_ids, probs, trade, gate_weight, up_weight, down_weight, out_grad):
    count, width = tokens.shape
    ff = gate_weight.shape[2]
    experts = lax.axis_size("expert")
    replicas = lax.axis_size("dp")
    chips = experts // 2
    share = width // replicas
    halfway = experts // 2
    numbers = jnp.arange(experts, dtype=jnp.int32)
    owners = jnp.where(
        jnp.concatenate([trade, trade]) == 1, jnp.bitwise_xor(numbers, halfway), numbers
    )
    weights = jnp.sum(
        jnp.where(expert_ids.T[None] == owners[:, None, None], probs.T[None], 0.0), axis=1
    )
    bf16, f32 = jnp.bfloat16, jnp.float32
    dma = pltpu.SemaphoreType.DMA
    total = experts * count
    hbm = pl.BlockSpec(memory_space=pl.ANY)
    vmem = pl.BlockSpec(memory_space=pltpu.VMEM)
    combined, gate, up, down = pl.pallas_call(
        layer_kernel,
        out_shape=(
            jax.ShapeDtypeStruct((count, width), bf16),
            jax.ShapeDtypeStruct((share, ff), bf16),
            jax.ShapeDtypeStruct((share, ff), bf16),
            jax.ShapeDtypeStruct((ff, share), bf16),
        ),
        in_specs=[hbm] * 6,
        out_specs=(vmem,) * 4,
        scratch_shapes=[
            pltpu.VMEM((experts, count, width), bf16),
            pltpu.VMEM((replicas, experts, count, share), bf16),
            pltpu.VMEM((experts, experts, count), f32),
            pltpu.VMEM((width, ff), bf16),
            pltpu.VMEM((width, ff), bf16),
            pltpu.VMEM((ff, width), bf16),
            pltpu.VMEM((total, count), f32),
            pltpu.VMEM((total, ff), bf16),
            pltpu.VMEM((total, 2 * ff), bf16),
            pltpu.VMEM((total, ff), f32),
            pltpu.VMEM((total, share), bf16),
            pltpu.VMEM((experts, count, width), bf16),
            pltpu.VMEM((chips, count, width), bf16),
            pltpu.VMEM((chips, count, width), bf16),
            pltpu.VMEM((replicas, share, 2 * ff), bf16),
            pltpu.VMEM((replicas, ff, share), bf16),
            pltpu.VMEM((2, share // 2, 2 * ff), bf16),
            pltpu.VMEM((2, share // 2, 2 * ff), bf16),
            pltpu.VMEM((2, ff // 2, share), bf16),
            pltpu.VMEM((2, ff // 2, share), bf16),
            pltpu.VMEM((2, share // 2, 2 * ff), bf16),
            pltpu.VMEM((2, ff // 2, share), bf16),
            dma((5 + replicas,)),
            dma((chips,)),
            dma((chips,)),
            dma((experts,)),
            dma((replicas, chips)),
            dma((replicas, chips)),
            dma((replicas, experts)),
            dma((experts,)),
            dma((experts,)),
            dma((chips,)),
            dma((chips,)),
            dma((chips,)),
            dma((chips,)),
            dma((12,)),
            dma((12,)),
        ],
        compiler_params=pltpu.CompilerParams(
            collective_id=0, has_side_effects=True, vmem_limit_bytes=67043328
        ),
    )(tokens, out_grad, weights, gate_weight[0], up_weight[0], down_weight[0])
    return combined, gate[None], up[None], down[None]


def local(tokens, expert_ids, *rest):
    experts, replicas = lax.axis_size("expert"), lax.axis_size("dp")
    capacity = 5 * tokens.shape[0] * expert_ids.shape[1] // (4 * experts)
    if tokens.shape[0] <= 2 * capacity and experts == 8 and replicas == 4:
        return chain_local(tokens, expert_ids, *rest)
    return sparse_local(tokens, expert_ids, *rest)


def solution(mesh):
    return jax.shard_map(
        local,
        mesh=mesh,
        in_specs=(
            P(("dp", "expert"), None),
            P(("dp", "expert"), None),
            P(("dp", "expert"), None),
            P(),
            P("expert", None, None),
            P("expert", None, None),
            P("expert", None, None),
            P(("dp", "expert"), None),
        ),
        out_specs=(
            P(("dp", "expert"), None),
            P("expert", "dp", None),
            P("expert", "dp", None),
            P("expert", None, "dp"),
        ),
        check_vma=False,
    )
```
